256 devices in a mesh: pipe: 16 (over z, core), dp: 2 (over y_hi), tensor: 8 (over y_lo, x).
Axes of the slice: x: 4, y: 4 (y_hi: 2, y_lo: 2; y = y_hi * 2 + y_lo), z: 8, core: 2. Of those that a mesh axis runs over, the one named last changes fastest.
Arguments:
- ssm_output: bfloat16 [16, 2, 1024, 8192], P('pipe', 'dp', None, 'tensor'), may hold values from -6 to 6
- out_weight: bfloat16 [16, 8192, 4096], P('pipe', 'tensor', 'dp'), may hold values from -0.0625 to 0.0625
- in_weight: bfloat16 [16, 4096, 2048], P('pipe', 'dp', 'tensor'), may hold values from -0.09375 to 0.09375
- gain: float32 [16, 4096], P('pipe'), may hold values from 0.1 to 1.9
- residual: bfloat16 [16, 2, 1024, 4096], P('pipe', 'dp', 'tensor'), may hold values from -1.5 to 1.5
- proj_cotangent: bfloat16 [16, 2, 1024, 2048], P('pipe', 'dp', None, 'tensor'), may hold values from -6 to 6
- stream_cotangent: bfloat16 [16, 2, 1024, 4096], P('pipe', 'dp', 'tensor'), may hold values from -12 to 12
Outputs:
- stream: bfloat16 [16, 2, 1024, 4096], P('pipe', 'dp', 'tensor')
- b_proj: bfloat16 [16, 2, 1024, 2048], P('pipe', 'dp', None, 'tensor')
- residual_grad: bfloat16 [16, 2, 1024, 4096], P('pipe', 'dp', 'tensor')
- gain_grad: float32 [16, 4096], P('pipe')
The draws below stay inside these ranges and needn't reach their ends.
All inputs are finite; a program needn't handle non-finite values.
Results may differ from the reference program's by a relative error of at most 0.014.
Values may be sent and summed in bfloat16 or wider, within the bound.
No kernel may reach another device: no remote copies, remote signals or barrier semaphores. Data moves between devices by JAX's collectives and lax.ppermute only.
A program may use at most 128 MiB of HBM per device.

```python
import math
import jax
import jax.numpy as jnp
from jax import lax

D = 4096
INNER = 8192
GS = 2048
LAYERS = 118
MB_TOK = 1024
SECTIONS = 16
SEQS = 2
N_TENSOR = 8


def block_levels(key, shape, shards, least, high):
    level, own = 1.0, jax.random.fold_in(key, 6)
    for dim, blocks in shards:
        draws = jnp.exp(jax.random.uniform(jax.random.fold_in(own, dim), (blocks,), jnp.float32, least / len(shards), high / len(shards)))
        level = level * jnp.repeat(draws, shape[dim] // blocks).reshape([-1 if axis == dim else 1 for axis in range(len(shape))])
    return level


def gaussian(rng, shape, width, bound, shards=(), kind=jnp.bfloat16):
    drawn = jax.random.normal(rng, shape, jnp.float32) * width
    if len(shards) > 0:
        drawn = block_levels(rng, shape, shards, -0.22, 0.18) * drawn
    return jnp.clip(drawn, min=-bound, max=bound).astype(kind)


def setup_inputs(seed: int = 0) -> dict:
    streams_of = jax.random.split(jax.random.key(seed), 8)
    return {
        "ssm_output": gaussian(streams_of[0], (SECTIONS, SEQS, MB_TOK, INNER), 1.0, 6.0, ((0, 16), (1, 2), (3, 8))),
        "out_weight": gaussian(streams_of[1], (SECTIONS, INNER, D), INNER ** -0.5, 0.0625, ((0, 16), (1, 8), (2, 2))),
        "in_weight": gaussian(streams_of[2], (SECTIONS, D, GS), D ** -0.5, 0.09375, ((0, 16), (1, 2), (2, 8))),
        "gain": jnp.clip(1.0 + 0.18 * jax.random.normal(streams_of[3], (SECTIONS, D), jnp.float32), 0.1, 1.9),
        "residual": gaussian(streams_of[4], (SECTIONS, SEQS, MB_TOK, D), 0.25, 1.5, ((0, 16), (1, 2), (2, 8))),
        "proj_cotangent": gaussian(streams_of[5], (SECTIONS, SEQS, MB_TOK, GS), 1.0, 6.0, ((0, 16), (1, 2), (3, 8))),
        "stream_cotangent": gaussian(streams_of[6], (SECTIONS, SEQS, MB_TOK, D), 2.0, 12.0, ((0, 16), (1, 2), (2, 8))),
    }


def rounded_sum(partials):
    narrow = lax.optimization_barrier(partials.astype(jnp.bfloat16))
    return lax.optimization_barrier(jnp.sum(narrow.astype(jnp.float32), axis=0))

def reference(ssm_output, out_weight, in_weight, gain, residual, proj_cotangent, stream_cotangent):
    depth_scale = 1.0 / math.sqrt(2.0 * LAYERS)
    width_inner = INNER // N_TENSOR
    width_cols = GS // N_TENSOR

    def mix_section(section_pair):
        ssm_rows, weight_out = section_pair
        blocked = ssm_rows.astype(jnp.float32).reshape(SEQS, MB_TOK, N_TENSOR, width_inner)
        weight_blocks = weight_out.astype(jnp.float32).reshape(N_TENSOR, width_inner, D)
        partials = jnp.einsum('stkc,kcd->kstd', blocked, weight_blocks)
        return rounded_sum(partials)
    mixed_sum = lax.map(mix_section, (ssm_output, out_weight))
    stream = (jnp.roll(residual, 1, 0).astype(jnp.float32) + depth_scale * jnp.roll(mixed_sum, 1, 0)).astype(jnp.bfloat16)

    def section_rest(section_items):
        stream_rows, gain_row, weight_in, cot_proj, cot_stream = section_items
        stream_f32 = stream_rows.astype(jnp.float32)
        inv_rms = lax.rsqrt(lax.optimization_barrier(jnp.mean(stream_f32 * stream_f32, axis=-1, keepdims=True)) + 1e-05)
        unit_rows = stream_f32 * inv_rms
        normed = (unit_rows * gain_row).astype(jnp.bfloat16)
        projected = jnp.einsum('std,dc->stc', normed.astype(jnp.float32), weight_in.astype(jnp.float32)).astype(jnp.bfloat16)
        cot_blocks = cot_proj.astype(jnp.float32).reshape(SEQS, MB_TOK, N_TENSOR, width_cols)
        weight_blocks = weight_in.astype(jnp.float32).reshape(D, N_TENSOR, width_cols)
        partials = jnp.einsum('stkc,dkc->kstd', cot_blocks, weight_blocks)
        normed_grad = rounded_sum(partials)
        gain_part = lax.optimization_barrier(jnp.sum(normed_grad * unit_rows, axis=(0, 1)))
        weighted = gain_row * normed_grad
        centre = lax.optimization_barrier(jnp.mean(weighted * unit_rows, axis=-1, keepdims=True))
        stream_grad = (cot_stream.astype(jnp.float32) + inv_rms * (weighted - unit_rows * centre)).astype(jnp.bfloat16)
        return (projected, stream_grad, gain_part)
    b_proj, stream_grad, gain_grad = lax.map(section_rest, (stream, gain, in_weight, proj_cotangent, stream_cotangent))
    residual_grad = jnp.roll(stream_grad, -1, 0)
    return (stream, b_proj, residual_grad, gain_grad)
```

```python
import math

import jax
import jax.numpy as jnp
from jax import lax
from jax.experimental import pallas as pl
from jax.experimental.pallas import tpu as pltpu
from jax.sharding import PartitionSpec as P


LAYERS = 118
NX = 4
NY = 4


PLANE = ("dp", "tensor")
ALL = ("pipe", "dp", "tensor")
f32 = jnp.float32
bf16 = jnp.bfloat16
shape = jax.ShapeDtypeStruct


def plane_route(to):
    return [
        (y * NX + x, (to(y, x)[0] % NY) * NX + to(y, x)[1] % NX)
        for y in range(NY)
        for x in range(NX)
    ]


RIGHT = plane_route(lambda y, x: (y, x + 1))
LEFT = plane_route(lambda y, x: (y, x - 1))
ACROSS = plane_route(lambda y, x: (y, x + 2))
PAIR = plane_route(lambda y, x: (y ^ 1, x))
CROSS = plane_route(lambda y, x: (3 - y, x))
REPLICA = plane_route(lambda y, x: (y + 2, x))
STAY = plane_route(lambda y, x: (y, x))


def move(block, route):
    return lax.ppermute(block, PLANE, route)


def ahead(block, route, distance=1):
    pipes = lax.axis_size("pipe")
    plane = NX * NY
    full = [
        (s * plane + a, ((s + distance) % pipes) * plane + b)
        for s in range(pipes)
        for a, b in route
    ]
    return lax.ppermute(block, ALL, full)


def after(block, *others):
    return lax.optimization_barrier((block, *others))[0]


def dot(a, b):
    return jnp.dot(a, b, preferred_element_type=f32)


def dot_t(a, b):
    return lax.dot_general(a, b, (((1,), (1,)), ((), ())), preferred_element_type=f32)


VMEM = pl.BlockSpec(memory_space=pltpu.VMEM)
SMEM = pl.BlockSpec(memory_space=pltpu.SMEM)


def run(kernel, out_shape, flops, moved, index, *args, scratch=()):
    count = len(out_shape) if isinstance(out_shape, list) else 1
    return pl.pallas_call(
        kernel,
        out_shape=out_shape,
        in_specs=[SMEM] + [VMEM] * len(args),
        out_specs=[VMEM] * count if count > 1 else VMEM,
        scratch_shapes=scratch,
        cost_estimate=pl.CostEstimate(flops=flops, bytes_accessed=moved, transcendentals=0),
        compiler_params=pltpu.CompilerParams(vmem_limit_bytes=24 << 20),
    )(index, *args)


HBM = pl.BlockSpec(memory_space=pltpu.HBM)


def load(parts, out_shape, index, arrays):
    def kernel(at, *refs):
        sources, outs, sems = refs[: len(arrays)], refs[len(arrays) : -1], refs[-1]
        copies = [
            pltpu.make_async_copy(a, b, sems.at[i])
            for i, (a, b) in enumerate(zip(parts(at, sources), outs))
        ]
        for copy in copies:
            copy.start()
        for copy in copies:
            copy.wait()

    return pl.pallas_call(
        kernel,
        out_shape=[shape(dims, bf16) for dims in out_shape],
        in_specs=[SMEM] + [HBM] * len(arrays),
        out_specs=[VMEM] * len(out_shape),
        scratch_shapes=[pltpu.SemaphoreType.DMA((len(out_shape),))],
        cost_estimate=pl.CostEstimate(
            flops=0, bytes_accessed=sum(4 * a.size for a in arrays), transcendentals=0
        ),
        compiler_params=pltpu.CompilerParams(vmem_limit_bytes=24 << 20),
    )(index, *arrays)


def add_terms(index, terms, dtype):
    def kernel(at, *refs):
        values = [ref[...].astype(f32) for ref in refs[:-1]]
        while len(values) > 1:
            values = [a + b for a, b in zip(values[::2], values[1::2])]
        refs[-1][...] = values[0].astype(dtype)

    return run(
        kernel, shape(terms[0].shape, dtype), terms[0].size, 8 * terms[0].size, index, *terms
    )


def back_products(index, cot, cot_pair, jobs):
    tokens = cot.shape[2]
    rows = jobs[0][1][0].shape[0]
    deep = min(256, rows)
    operands, plan = [], []
    for step, mine, theirs, adds, dtype in jobs:
        spots = []
        for array in (*mine, *theirs, *adds):
            known = [i for i, o in enumerate(operands) if o is array]
            if not known:
                operands.append(array)
            spots.append(known[0] if known else len(operands) - 1)
        plan.append((step, spots, dtype))

    def kernel(at, cot_ref, pair_ref, *refs):
        outs = refs[len(operands) :]
        for (step, spots, dtype), out in zip(plan, outs):
            a, b = cot_ref[at[4], at[step]], pair_ref[at[step]]
            for i in range(2):

                @pl.loop(0, rows // deep)
                def _(n):
                    own = pl.ds(pl.multiple_of(n * deep, deep), deep)
                    cols = pl.ds(pl.multiple_of(i * rows + n * deep, deep), deep)
                    value = dot_t(a, refs[spots[i]][own]) + dot_t(b, refs[spots[2 + i]][own])
                    for spot in spots[4:]:
                        value = value + refs[spot][:, cols].astype(f32)
                    out[:, cols] = value.astype(dtype)


    return run(
        kernel,
        [shape((tokens, 2 * rows), dtype) for _, _, dtype in plan],
        len(jobs) * 8 * tokens * cot.shape[3] * rows,
        sum(4 * o.size for o in operands),
        index,
        cot,
        cot_pair,
        *operands,
    )


def store(block):
    def kernel(block_ref, out_ref, sem):
        copy = pltpu.make_async_copy(block_ref, out_ref, sem)
        copy.start()
        copy.wait()

    return pl.pallas_call(
        kernel,
        out_shape=shape(block.shape, block.dtype),
        in_specs=[VMEM],
        out_specs=pl.BlockSpec(memory_space=pl.ANY),
        scratch_shapes=[pltpu.SemaphoreType.DMA],
        cost_estimate=pl.CostEstimate(flops=0, bytes_accessed=4 * block.size, transcendentals=0),
        compiler_params=pltpu.CompilerParams(vmem_limit_bytes=12 << 20),
        name="st",
    )(block)


def row_products(part, rows, steps, index, w, adds, choose=False):
    tokens, channels = part[0].shape[-2:]
    columns = w.shape[1]
    wide = min(512, columns)
    first = len(adds[0])

    def kernel(at, one_ref, two_ref, w_ref, *rest):
        add_refs, (p_ref, q_ref, both) = rest[:-3], rest[-3:]
        both[:tokens] = one_ref[at[steps[0]]]
        both[tokens:] = two_ref[at[steps[1]]]

        def step(n):
            cols = pl.ds(pl.multiple_of(n * wide, wide), wide)
            product = dot(both[...], w_ref[:, cols])
            p, q = product[:tokens], product[tokens:]
            for ref in add_refs[:first]:
                p = p + ref[:, cols].astype(f32)
            for ref in add_refs[first:]:
                q = q + ref[:, cols].astype(f32)
            if choose:
                swap = at[4] != 0
                p, q = jnp.where(swap, q, p), jnp.where(swap, p, q)
            p_ref[:, cols] = p.astype(bf16)
            q_ref[:, cols] = q.astype(bf16)

        pl.loop(0, columns // wide)(step)

    extra = list(adds[0]) + list(adds[1])
    return run(
        kernel,
        [shape((tokens, columns), bf16)] * 2,
        4 * tokens * channels * columns,
        2 * channels * columns + 4 * tokens * (channels + columns),
        index,
        part[rows[0]],
        part[rows[1]],
        w,
        *extra,
        scratch=[pltpu.VMEM((2 * tokens, channels), bf16)],
    )


def stream_and_norm(index, resid, keep, passed, crossed, gain, depth_scale):
    tokens, width = resid.shape
    half = width // 2
    rows = min(16, tokens)

    def kernel(at, r_ref, k_ref, p_ref, c_ref, g_ref, s_ref, nd, no, inv_ref):
        to_d = pl.ds(pl.multiple_of(at[5] * half, half), half)
        to_o = pl.ds(pl.multiple_of(at[6] * half, half), half)

        @pl.loop(0, tokens // rows)
        def _(n):
            r = pl.ds(pl.multiple_of(n * rows, rows), rows)
            sd = k_ref[r].astype(f32) + p_ref[r].astype(f32)
            sd = (r_ref[r, to_d].astype(f32) + depth_scale * sd).astype(bf16)
            so = (r_ref[r, to_o].astype(f32) + depth_scale * c_ref[r].astype(f32)).astype(bf16)
            s_ref[r, to_d] = sd
            s_ref[r, to_o] = so
            sd, so = sd.astype(f32), so.astype(f32)
            square = jnp.sum(sd * sd + so * so, axis=-1, keepdims=True)
            inv = lax.rsqrt(square / width + 1e-05)
            inv_ref[r] = inv
            nd[r] = (sd * inv * g_ref[:, to_d]).astype(bf16)
            no[r] = (so * inv * g_ref[:, to_o]).astype(bf16)

    return run(
        kernel,
        [
            shape((tokens, width), bf16),
            shape((tokens, half), bf16),
            shape((tokens, half), bf16),
            shape((tokens, 1), f32),
        ],
        12 * tokens * width,
        8 * tokens * width,
        index,
        resid,
        keep,
        passed,
        crossed,
        gain,
    )


def norm_backward(index, stream, inv, cot, gain, grad_d, grad_o):
    tokens, width = stream.shape
    half = width // 2
    rows = min(16, tokens)

    def kernel(at, s_ref, inv_ref, c_ref, g_ref, h0, h1, h2, h3, h4, h5, out, total):
        to_d = pl.ds(pl.multiple_of(at[5] * half, half), half)
        to_o = pl.ds(pl.multiple_of(at[6] * half, half), half)
        total[...] = jnp.zeros_like(total)

        @pl.loop(0, tokens // rows)
        def _(n):
            r = pl.ds(pl.multiple_of(n * rows, rows), rows)
            inv = inv_ref[r]
            hd = h0[r] + h1[r].astype(f32) + h2[r].astype(f32)
            ho = h3[r] + h4[r].astype(f32) + h5[r].astype(f32)
            ud, uo = s_ref[r, to_d].astype(f32) * inv, s_ref[r, to_o].astype(f32) * inv
            wd, wo = g_ref[:, to_d] * hd, g_ref[:, to_o] * ho
            centre = jnp.sum(wd * ud + wo * uo, axis=-1, keepdims=True) / width
            out[r, to_d] = (c_ref[r, to_d].astype(f32) + inv * (wd - ud * centre)).astype(bf16)
            out[r, to_o] = (c_ref[r, to_o].astype(f32) + inv * (wo - uo * centre)).astype(bf16)
            total[:, to_d] += jnp.sum(hd * ud, axis=0, keepdims=True)
            total[:, to_o] += jnp.sum(ho * uo, axis=0, keepdims=True)

    return run(
        kernel,
        [shape((tokens, width), bf16), shape((1, width), f32)],
        16 * tokens * width,
        16 * tokens * width,
        index,
        stream,
        inv,
        cot,
        gain,
        *grad_d,
        *grad_o,
    )


def project(index, blocks, weights):
    count = len(blocks)
    tokens, half = blocks[0][0].shape
    rows, columns = weights[0].shape

    def kernel(at, *refs):
        w, (mine, send), held = refs[2 * count : -3], refs[-3:-1], refs[-1]
        for i in range(count):
            held[i, 0] = refs[2 * i][...]
            held[i, 1] = refs[2 * i + 1][...]

        @pl.loop(0, count)
        def _(i):
            for out, first in ((send, 4), (mine, 0)):
                total = dot(held[i, 0, :, :rows], w[first][...])
                total = total + dot(held[i, 0, :, rows:], w[first + 1][...])
                total = total + dot(held[i, 1, :, :rows], w[first + 2][...])
                total = total + dot(held[i, 1, :, rows:], w[first + 3][...])
                out[i] = total.astype(bf16)

    return run(
        kernel,
        [shape((count, tokens, columns), bf16)] * 2,
        8 * count * tokens * half * columns,
        8 * half * columns + 4 * count * tokens * (half + columns),
        index,
        *[a for pair in blocks for a in pair],
        *weights,
        scratch=[pltpu.VMEM((count, 2, tokens, half), bf16)],
    )


def place(index, mine3, mine1, theirs3, theirs1):
    tokens, columns = mine3.shape[1:]

    def kernel(at, a3, a1, b3, b1, out):
        for row, three, one in ((at[4], a3, a1), (1 - at[4], b3, b1)):
            for slot, step in enumerate((0, 1, 3)):
                out[row, at[step]] = three[slot]
            out[row, at[2]] = one[0]

    return run(
        kernel,
        shape((2, NX, tokens, columns), bf16),
        0,
        32 * tokens * columns,
        index,
        mine3,
        mine1,
        theirs3,
        theirs1,
    )


def compute(ssm_output, out_weight, in_weight, gain, residual, proj_cotangent, stream_cotangent):
    depth_scale = 1.0 / math.sqrt(2.0 * LAYERS)
    d = lax.axis_index("dp").astype(jnp.int32)
    t = lax.axis_index("tensor").astype(jnp.int32)
    lane_row = t // NX
    x = t % NX
    resid = residual[0, 0]
    cot_stream = stream_cotangent[0, 0]
    ssm = ssm_output[0, 0]
    tokens = ssm.shape[0]
    block = tokens // 8
    index = jnp.stack([x, (x + 1) % NX, (x + 2) % NX, (x + 3) % NX, lane_row, d, 1 - d, 0 * d])

    ssm = ssm.reshape(2, NX, block, -1)
    cot = proj_cotangent[0, 0].reshape(2, NX, block, -1)
    w_out, w_in = out_weight[0], in_weight[0]
    own = load(lambda at, refs: [refs[0].at[0], refs[0].at[1]], [ssm.shape[1:]] * 2, index, [ssm])
    other = [move(own[0], REPLICA), move(own[1], REPLICA)]
    resid_in = ahead(resid, STAY)
    order = []

    def product(part, rows, steps, adds):
        at = after(index, *order[-1:])
        a, b = row_products(part, rows, steps, at, w_out, adds, steps == (0, 0))
        order.append(a)
        return a, b

    def reduce_start(part):
        far_r, far_l = product(part, (0, 1), (2, 2), ((), ()))
        far_r, far_l = move(far_r, RIGHT), move(far_l, LEFT)
        l0, r1 = product(part, (0, 1), (3, 1), ((), ()))
        return far_r, far_l, move(l0, LEFT), move(r1, RIGHT)

    def reduce_relay(part, started):
        far_r, far_l, l0, r1 = started
        r0, l1 = product(part, (0, 1), (1, 3), ((far_r,), (far_l,)))
        r0, l1 = move(r0, RIGHT), move(l1, LEFT)
        return (l0, r0), (r1, l1)

    def reduce_end(part, arrived):
        return product(part, (0, 1), (0, 0), arrived)

    started = reduce_start(own)
    rows = w_in.shape[0] // 2
    w_a, w_b, cot, cot_send = load(
        lambda at, refs: [
            refs[0].at[pl.ds(0, rows)],
            refs[0].at[pl.ds(rows, rows)],
            refs[1],
            refs[1].at[1 - at[4]],
        ],
        [(rows, w_in.shape[1])] * 2 + [cot.shape, cot.shape[1:]],
        after(index, order[-1]),
        [w_in, cot],
    )
    cot_pair = move(cot_send, PAIR)
    own_arrived = reduce_relay(own, started)
    far_r, l0 = product(other, (0, 0), (2, 3), ((), ()))
    far_r, l0 = move(far_r, RIGHT), move(l0, LEFT)
    far_l, r1 = product(other, (1, 1), (2, 1), ((), ()))
    far_l, r1 = move(far_l, LEFT), move(r1, RIGHT)
    started = far_r, far_l, l0, r1
    keep, pass_on = reduce_end(own, own_arrived)
    keep = ahead(keep, STAY)
    pass_on = ahead(pass_on, PAIR)
    oth_arrived = reduce_relay(other, started)
    to_pair, crossing = reduce_end(other, oth_arrived)
    to_pair = move(to_pair, PAIR)
    crossing = add_terms(index, (crossing, to_pair), bf16)
    crossing = ahead(crossing, CROSS)

    pair_a, cross_b = move(after(w_a, other[1]), PAIR), move(w_b, CROSS)
    pair_b, cross_a = move(w_b, PAIR), move(w_a, CROSS)
    opp_a, opp_b = move(pair_a, CROSS), move(cross_b, PAIR)

    half_d = ((w_a, w_b), (pair_a, pair_b))
    half_o = ((opp_a, opp_b), (cross_a, cross_b))

    def back(jobs):
        return back_products(index, cot, cot_pair, jobs)

    far_r, l0 = back([(2, *half_d, (), bf16), (3, *half_d, (), bf16)])
    far_r, l0 = move(far_r, RIGHT), move(l0, LEFT)
    far_l, r1 = back([(2, *half_o, (), bf16), (1, *half_o, (), bf16)])
    far_l, r1 = move(far_l, LEFT), move(r1, RIGHT)
    r0, l1 = back([(1, *half_d, (far_r,), bf16), (3, *half_o, (far_l,), bf16)])
    r0, l1 = move(r0, RIGHT), move(l1, LEFT)
    grad_d, grad_o = back([(0, *half_d, (), f32), (0, *half_o, (), f32)])

    stream, norm_d, norm_o, inv_rms = stream_and_norm(
        index, resid_in, keep, pass_on, crossing, gain, depth_scale
    )

    d_l, o_r = move(norm_d, RIGHT), move(norm_o, LEFT)
    d_r, o_l = move(norm_d, LEFT), move(norm_o, RIGHT)
    d_f, o_f = move(d_l, RIGHT), move(o_r, LEFT)
    stream_grad, gain_part = norm_backward(
        index, stream, inv_rms, cot_stream, gain, (grad_d, l0, r0), (grad_o, r1, l1)
    )
    resid_grad = store(ahead(stream_grad, STAY, -1))
    for routes in ((ACROSS, RIGHT, LEFT), (REPLICA, PAIR, CROSS)):
        a, b, c = (move(gain_part, r) for r in routes)
        gain_part = add_terms(index, (gain_part, a, b, c), f32)

    weights = (w_a, w_b, opp_a, opp_b, pair_a, pair_b, cross_a, cross_b)
    mine3, send3 = project(index, [(norm_d, norm_o), (d_r, o_r), (d_l, o_l)], weights)
    theirs3 = move(send3, PAIR)
    mine1, send1 = project(index, [(d_f, o_f)], weights)
    theirs1 = move(send1, PAIR)
    projected = place(after(index, resid_grad, gain_part), mine3, mine1, theirs3, theirs1)
    projected = projected.reshape(tokens, -1)

    return stream[None, None], projected[None, None], resid_grad[None, None], gain_part


def solution(mesh):
    in_specs = (
        P("pipe", "dp", None, "tensor"),
        P("pipe", "tensor", "dp"),
        P("pipe", "dp", "tensor"),
        P("pipe", None),
        P("pipe", "dp", "tensor", None),
        P("pipe", "dp", None, "tensor"),
        P("pipe", "dp", "tensor", None),
    )
    out_specs = (
        P("pipe", "dp", "tensor", None),
        P("pipe", "dp", None, "tensor"),
        P("pipe", "dp", "tensor", None),
        P("pipe", None),
    )
    return jax.shard_map(compute, mesh=mesh, in_specs=in_specs, out_specs=out_specs, check_vma=False)
```

```python
import math

import jax
import jax.numpy as jnp
from jax import lax
from jax.experimental import pallas as pl
from jax.experimental.pallas import tpu as pltpu
from jax.sharding import PartitionSpec as P


LAYERS = 118
NX = 4
NY = 4


PLANE = ("dp", "tensor")
ALL = ("pipe", "dp", "tensor")
f32 = jnp.float32
bf16 = jnp.bfloat16
shape = jax.ShapeDtypeStruct


def plane_route(to):
    return [
        (y * NX + x, (to(y, x)[0] % NY) * NX + to(y, x)[1] % NX)
        for y in range(NY)
        for x in range(NX)
    ]


RIGHT = plane_route(lambda y, x: (y, x + 1))
LEFT = plane_route(lambda y, x: (y, x - 1))
ACROSS = plane_route(lambda y, x: (y, x + 2))
PAIR = plane_route(lambda y, x: (y ^ 1, x))
CROSS = plane_route(lambda y, x: (3 - y, x))
REPLICA = plane_route(lambda y, x: (y + 2, x))
STAY = plane_route(lambda y, x: (y, x))


def move(block, route):
    return lax.ppermute(block, PLANE, route)


def ahead(block, route, distance=1):
    pipes = lax.axis_size("pipe")
    plane = NX * NY
    full = [
        (s * plane + a, ((s + distance) % pipes) * plane + b)
        for s in range(pipes)
        for a, b in route
    ]
    return lax.ppermute(block, ALL, full)


def after(block, *others):
    return lax.optimization_barrier((block, *others))[0]


def dot(a, b):
    return jnp.dot(a, b, preferred_element_type=f32)


def dot_t(a, b):
    return lax.dot_general(a, b, (((1,), (1,)), ((), ())), preferred_element_type=f32)


VMEM = pl.BlockSpec(memory_space=pltpu.VMEM)
SMEM = pl.BlockSpec(memory_space=pltpu.SMEM)


def run(kernel, out_shape, flops, moved, index, *args, scratch=()):
    count = len(out_shape) if isinstance(out_shape, list) else 1
    return pl.pallas_call(
        kernel,
        out_shape=out_shape,
        in_specs=[SMEM] + [VMEM] * len(args),
        out_specs=[VMEM] * count if count > 1 else VMEM,
        scratch_shapes=scratch,
        cost_estimate=pl.CostEstimate(flops=flops, bytes_accessed=moved, transcendentals=0),
        compiler_params=pltpu.CompilerParams(vmem_limit_bytes=24 << 20),
    )(index, *args)


HBM = pl.BlockSpec(memory_space=pltpu.HBM)


def load(parts, out_shape, index, arrays):
    def kernel(at, *refs):
        sources, outs, sems = refs[: len(arrays)], refs[len(arrays) : -1], refs[-1]
        copies = [
            pltpu.make_async_copy(a, b, sems.at[i])
            for i, (a, b) in enumerate(zip(parts(at, sources), outs))
        ]
        for copy in copies:
            copy.start()
        for copy in copies:
            copy.wait()

    return pl.pallas_call(
        kernel,
        out_shape=[shape(dims, bf16) for dims in out_shape],
        in_specs=[SMEM] + [HBM] * len(arrays),
        out_specs=[VMEM] * len(out_shape),
        scratch_shapes=[pltpu.SemaphoreType.DMA((len(out_shape),))],
        cost_estimate=pl.CostEstimate(
            flops=0, bytes_accessed=sum(4 * a.size for a in arrays), transcendentals=0
        ),
        compiler_params=pltpu.CompilerParams(vmem_limit_bytes=24 << 20),
    )(index, *arrays)


def add_terms(index, terms, dtype):
    def kernel(at, *refs):
        values = [ref[...].astype(f32) for ref in refs[:-1]]
        while len(values) > 1:
            values = [a + b for a, b in zip(values[::2], values[1::2])]
        refs[-1][...] = values[0].astype(dtype)

    return run(
        kernel, shape(terms[0].shape, dtype), terms[0].size, 8 * terms[0].size, index, *terms
    )


def back_products(index, cot, cot_pair, jobs, deep=256):
    tokens = cot.shape[2]
    rows = jobs[0][1][0].shape[0]
    deep = min(deep, rows)
    operands, plan = [], []
    for step, mine, theirs, adds, dtype in jobs:
        spots = []
        for array in (*mine, *theirs, *adds):
            known = [i for i, o in enumerate(operands) if o is array]
            if not known:
                operands.append(array)
            spots.append(known[0] if known else len(operands) - 1)
        plan.append((step, spots, dtype))

    together = len(jobs) == 2 and plan[0][1] == plan[1][1] and len(plan[0][1]) == 4

    def kernel(at, cot_ref, pair_ref, *refs):
        outs = refs[len(operands) :]
        if together:
            steps, spots = [at[step] for step, _, _ in plan], plan[0][1]
            a = jnp.concatenate([cot_ref[at[4], step] for step in steps], axis=0)
            b = jnp.concatenate([pair_ref[step] for step in steps], axis=0)
            for i in range(2):

                @pl.loop(0, rows // deep)
                def _(n):
                    own = pl.ds(pl.multiple_of(n * deep, deep), deep)
                    cols = pl.ds(pl.multiple_of(i * rows + n * deep, deep), deep)
                    value = dot_t(a, refs[spots[i]][own]) + dot_t(b, refs[spots[2 + i]][own])
                    outs[0][:, cols] = value[:tokens].astype(plan[0][2])
                    outs[1][:, cols] = value[tokens:].astype(plan[1][2])

            return
        for (step, spots, dtype), out in zip(plan, outs):
            a, b = cot_ref[at[4], at[step]], pair_ref[at[step]]
            for i in range(2):

                @pl.loop(0, rows // deep)
                def _(n):
                    own = pl.ds(pl.multiple_of(n * deep, deep), deep)
                    cols = pl.ds(pl.multiple_of(i * rows + n * deep, deep), deep)
                    value = dot_t(a, refs[spots[i]][own]) + dot_t(b, refs[spots[2 + i]][own])
                    for spot in spots[4:]:
                        value = value + refs[spot][:, cols].astype(f32)
                    out[:, cols] = value.astype(dtype)


    return run(
        kernel,
        [shape((tokens, 2 * rows), dtype) for _, _, dtype in plan],
        len(jobs) * 8 * tokens * cot.shape[3] * rows,
        sum(4 * o.size for o in operands),
        index,
        cot,
        cot_pair,
        *operands,
    )


def store(block):
    def kernel(block_ref, out_ref, sem):
        copy = pltpu.make_async_copy(block_ref, out_ref, sem)
        copy.start()
        copy.wait()

    return pl.pallas_call(
        kernel,
        out_shape=shape(block.shape, block.dtype),
        in_specs=[VMEM],
        out_specs=pl.BlockSpec(memory_space=pl.ANY),
        scratch_shapes=[pltpu.SemaphoreType.DMA],
        cost_estimate=pl.CostEstimate(flops=0, bytes_accessed=4 * block.size, transcendentals=0),
        compiler_params=pltpu.CompilerParams(vmem_limit_bytes=12 << 20),
        name="st",
    )(block)


def row_products(part, rows, steps, index, w, adds, choose=False):
    tokens, channels = part[0].shape[-2:]
    columns = w.shape[1]
    wide = min(512, columns)
    first = len(adds[0])

    def kernel(at, one_ref, two_ref, w_ref, *rest):
        add_refs, (p_ref, q_ref, both) = rest[:-3], rest[-3:]
        both[:tokens] = one_ref[at[steps[0]]]
        both[tokens:] = two_ref[at[steps[1]]]

        def step(n):
            cols = pl.ds(pl.multiple_of(n * wide, wide), wide)
            product = dot(both[...], w_ref[:, cols])
            p, q = product[:tokens], product[tokens:]
            for ref in add_refs[:first]:
                p = p + ref[:, cols].astype(f32)
            for ref in add_refs[first:]:
                q = q + ref[:, cols].astype(f32)
            if choose:
                swap = at[4] != 0
                p, q = jnp.where(swap, q, p), jnp.where(swap, p, q)
            p_ref[:, cols] = p.astype(bf16)
            q_ref[:, cols] = q.astype(bf16)

        pl.loop(0, columns // wide)(step)

    extra = list(adds[0]) + list(adds[1])
    return run(
        kernel,
        [shape((tokens, columns), bf16)] * 2,
        4 * tokens * channels * columns,
        2 * channels * columns + 4 * tokens * (channels + columns),
        index,
        part[rows[0]],
        part[rows[1]],
        w,
        *extra,
        scratch=[pltpu.VMEM((2 * tokens, channels), bf16)],
    )


def stream_and_norm(index, resid, keep, passed, crossed, gain, depth_scale):
    tokens, width = resid.shape
    half = width // 2
    rows = min(16, tokens)

    def kernel(at, r_ref, k_ref, p_ref, c_ref, g_ref, s_ref, nd, no, inv_ref):
        to_d = pl.ds(pl.multiple_of(at[5] * half, half), half)
        to_o = pl.ds(pl.multiple_of(at[6] * half, half), half)

        @pl.loop(0, tokens // rows)
        def _(n):
            r = pl.ds(pl.multiple_of(n * rows, rows), rows)
            sd = k_ref[r].astype(f32) + p_ref[r].astype(f32)
            sd = (r_ref[r, to_d].astype(f32) + depth_scale * sd).astype(bf16)
            so = (r_ref[r, to_o].astype(f32) + depth_scale * c_ref[r].astype(f32)).astype(bf16)
            s_ref[r, to_d] = sd
            s_ref[r, to_o] = so
            sd, so = sd.astype(f32), so.astype(f32)
            square = jnp.sum(sd * sd + so * so, axis=-1, keepdims=True)
            inv = lax.rsqrt(square / width + 1e-05)
            inv_ref[r] = inv
            nd[r] = (sd * inv * g_ref[:, to_d]).astype(bf16)
            no[r] = (so * inv * g_ref[:, to_o]).astype(bf16)

    return run(
        kernel,
        [
            shape((tokens, width), bf16),
            shape((tokens, half), bf16),
            shape((tokens, half), bf16),
            shape((tokens, 1), f32),
        ],
        12 * tokens * width,
        8 * tokens * width,
        index,
        resid,
        keep,
        passed,
        crossed,
        gain,
    )


def norm_backward(index, stream, inv, cot, gain, grad_d, grad_o):
    tokens, width = stream.shape
    half = width // 2
    rows = min(16, tokens)

    def kernel(at, s_ref, inv_ref, c_ref, g_ref, h0, h1, h2, h3, h4, h5, out, total):
        to_d = pl.ds(pl.multiple_of(at[5] * half, half), half)
        to_o = pl.ds(pl.multiple_of(at[6] * half, half), half)
        total[...] = jnp.zeros_like(total)

        @pl.loop(0, tokens // rows)
        def _(n):
            r = pl.ds(pl.multiple_of(n * rows, rows), rows)
            inv = inv_ref[r]
            hd = h0[r] + h1[r].astype(f32) + h2[r].astype(f32)
            ho = h3[r] + h4[r].astype(f32) + h5[r].astype(f32)
            ud, uo = s_ref[r, to_d].astype(f32) * inv, s_ref[r, to_o].astype(f32) * inv
            wd, wo = g_ref[:, to_d] * hd, g_ref[:, to_o] * ho
            centre = jnp.sum(wd * ud + wo * uo, axis=-1, keepdims=True) / width
            out[r, to_d] = (c_ref[r, to_d].astype(f32) + inv * (wd - ud * centre)).astype(bf16)
            out[r, to_o] = (c_ref[r, to_o].astype(f32) + inv * (wo - uo * centre)).astype(bf16)
            total[:, to_d] += jnp.sum(hd * ud, axis=0, keepdims=True)
            total[:, to_o] += jnp.sum(ho * uo, axis=0, keepdims=True)

    return run(
        kernel,
        [shape((tokens, width), bf16), shape((1, width), f32)],
        16 * tokens * width,
        16 * tokens * width,
        index,
        stream,
        inv,
        cot,
        gain,
        *grad_d,
        *grad_o,
    )


def project(index, blocks, weights):
    count = len(blocks)
    tokens, half = blocks[0][0].shape
    rows, columns = weights[0].shape

    def kernel(at, *refs):
        w, (mine, send), held = refs[2 * count : -3], refs[-3:-1], refs[-1]
        for i in range(count):
            held[i, 0] = refs[2 * i][...]
            held[i, 1] = refs[2 * i + 1][...]

        @pl.loop(0, count)
        def _(i):
            for out, first in ((send, 4), (mine, 0)):
                total = dot(held[i, 0, :, :rows], w[first][...])
                total = total + dot(held[i, 0, :, rows:], w[first + 1][...])
                total = total + dot(held[i, 1, :, :rows], w[first + 2][...])
                total = total + dot(held[i, 1, :, rows:], w[first + 3][...])
                out[i] = total.astype(bf16)

    return run(
        kernel,
        [shape((count, tokens, columns), bf16)] * 2,
        8 * count * tokens * half * columns,
        8 * half * columns + 4 * count * tokens * (half + columns),
        index,
        *[a for pair in blocks for a in pair],
        *weights,
        scratch=[pltpu.VMEM((count, 2, tokens, half), bf16)],
    )


def place(index, mine3, mine1, theirs3, theirs1):
    tokens, columns = mine3.shape[1:]

    def kernel(at, a3, a1, b3, b1, out):
        for row, three, one in ((at[4], a3, a1), (1 - at[4], b3, b1)):
            for slot, step in enumerate((0, 1, 3)):
                out[row, at[step]] = three[slot]
            out[row, at[2]] = one[0]

    return run(
        kernel,
        shape((2, NX, tokens, columns), bf16),
        0,
        32 * tokens * columns,
        index,
        mine3,
        mine1,
        theirs3,
        theirs1,
    )


def compute(ssm_output, out_weight, in_weight, gain, residual, proj_cotangent, stream_cotangent):
    depth_scale = 1.0 / math.sqrt(2.0 * LAYERS)
    d = lax.axis_index("dp").astype(jnp.int32)
    t = lax.axis_index("tensor").astype(jnp.int32)
    lane_row = t // NX
    x = t % NX
    resid = residual[0, 0]
    cot_stream = stream_cotangent[0, 0]
    ssm = ssm_output[0, 0]
    tokens = ssm.shape[0]
    block = tokens // 8
    index = jnp.stack([x, (x + 1) % NX, (x + 2) % NX, (x + 3) % NX, lane_row, d, 1 - d, 0 * d])

    ssm = ssm.reshape(2, NX, block, -1)
    cot = proj_cotangent[0, 0].reshape(2, NX, block, -1)
    w_out, w_in = out_weight[0], in_weight[0]
    own = load(lambda at, refs: [refs[0].at[0], refs[0].at[1]], [ssm.shape[1:]] * 2, index, [ssm])
    other = [move(own[0], REPLICA), move(own[1], REPLICA)]
    resid_in = ahead(resid, STAY)
    order = []

    def product(part, rows, steps, adds):
        at = after(index, *order[-1:])
        a, b = row_products(part, rows, steps, at, w_out, adds, steps == (0, 0))
        order.append(a)
        return a, b

    def reduce_start(part):
        far_r, far_l = product(part, (0, 1), (2, 2), ((), ()))
        far_r, far_l = move(far_r, RIGHT), move(far_l, LEFT)
        l0, r1 = product(part, (0, 1), (3, 1), ((), ()))
        return far_r, far_l, move(l0, LEFT), move(r1, RIGHT)

    def reduce_relay(part, started):
        far_r, far_l, l0, r1 = started
        r0, l1 = product(part, (0, 1), (1, 3), ((far_r,), (far_l,)))
        r0, l1 = move(r0, RIGHT), move(l1, LEFT)
        return (l0, r0), (r1, l1)

    def reduce_end(part, arrived):
        return product(part, (0, 1), (0, 0), arrived)

    started = reduce_start(own)
    rows = w_in.shape[0] // 2
    w_a, w_b, cot, cot_send = load(
        lambda at, refs: [
            refs[0].at[pl.ds(0, rows)],
            refs[0].at[pl.ds(rows, rows)],
            refs[1],
            refs[1].at[1 - at[4]],
        ],
        [(rows, w_in.shape[1])] * 2 + [cot.shape, cot.shape[1:]],
        after(index, order[-1]),
        [w_in, cot],
    )
    cot_pair = move(cot_send, PAIR)
    own_arrived = reduce_relay(own, started)
    far_r, l0 = product(other, (0, 0), (2, 3), ((), ()))
    far_r, l0 = move(far_r, RIGHT), move(l0, LEFT)
    far_l, r1 = product(other, (1, 1), (2, 1), ((), ()))
    far_l, r1 = move(far_l, LEFT), move(r1, RIGHT)
    started = far_r, far_l, l0, r1
    keep, pass_on = reduce_end(own, own_arrived)
    keep = ahead(keep, STAY)
    pass_on = ahead(pass_on, PAIR)
    oth_arrived = reduce_relay(other, started)
    to_pair, crossing = reduce_end(other, oth_arrived)
    to_pair = move(to_pair, PAIR)
    crossing = add_terms(index, (crossing, to_pair), bf16)
    crossing = ahead(crossing, CROSS)

    pair_a, cross_b = move(after(w_a, other[1]), PAIR), move(w_b, CROSS)
    pair_b, cross_a = move(w_b, PAIR), move(w_a, CROSS)
    opp_a, opp_b = move(pair_a, CROSS), move(cross_b, PAIR)

    half_d = ((w_a, w_b), (pair_a, pair_b))
    half_o = ((opp_a, opp_b), (cross_a, cross_b))

    def back(jobs, deep=256):
        return back_products(index, cot, cot_pair, jobs, deep)

    far_r, l0 = back([(2, *half_d, (), bf16), (3, *half_d, (), bf16)])
    far_r, l0 = move(far_r, RIGHT), move(l0, LEFT)
    far_l, r1 = back([(2, *half_o, (), bf16), (1, *half_o, (), bf16)])
    far_l, r1 = move(far_l, LEFT), move(r1, RIGHT)
    r0, l1 = back([(1, *half_d, (far_r,), bf16), (3, *half_o, (far_l,), bf16)], 512)
    r0, l1 = move(r0, RIGHT), move(l1, LEFT)
    grad_d, grad_o = back([(0, *half_d, (), f32), (0, *half_o, (), f32)])

    stream, norm_d, norm_o, inv_rms = stream_and_norm(
        index, resid_in, keep, pass_on, crossing, gain, depth_scale
    )

    d_l, o_r = move(norm_d, RIGHT), move(norm_o, LEFT)
    d_r, o_l = move(norm_d, LEFT), move(norm_o, RIGHT)
    d_f, o_f = move(d_l, RIGHT), move(o_r, LEFT)
    stream_grad, gain_part = norm_backward(
        index, stream, inv_rms, cot_stream, gain, (grad_d, l0, r0), (grad_o, r1, l1)
    )
    resid_grad = store(ahead(stream_grad, STAY, -1))
    for routes in ((ACROSS, RIGHT, LEFT), (REPLICA, PAIR, CROSS)):
        a, b, c = (move(gain_part, r) for r in routes)
        gain_part = add_terms(index, (gain_part, a, b, c), f32)

    weights = (w_a, w_b, opp_a, opp_b, pair_a, pair_b, cross_a, cross_b)
    mine3, send3 = project(index, [(norm_d, norm_o), (d_r, o_r), (d_l, o_l)], weights)
    theirs3 = move(send3, PAIR)
    mine1, send1 = project(index, [(d_f, o_f)], weights)
    theirs1 = move(send1, PAIR)
    projected = place(after(index, resid_grad, gain_part), mine3, mine1, theirs3, theirs1)
    projected = projected.reshape(tokens, -1)

    return stream[None, None], projected[None, None], resid_grad[None, None], gain_part


def solution(mesh):
    in_specs = (
        P("pipe", "dp", None, "tensor"),
        P("pipe", "tensor", "dp"),
        P("pipe", "dp", "tensor"),
        P("pipe", None),
        P("pipe", "dp", "tensor", None),
        P("pipe", "dp", None, "tensor"),
        P("pipe", "dp", "tensor", None),
    )
    out_specs = (
        P("pipe", "dp", "tensor", None),
        P("pipe", "dp", None, "tensor"),
        P("pipe", "dp", "tensor", None),
        P("pipe", None),
    )
    return jax.shard_map(compute, mesh=mesh, in_specs=in_specs, out_specs=out_specs, check_vma=False)
```
